32 devices in a mesh: rows: 4 (over y, x), cols: 8 (over z, core).
Axes of the slice: x: 2, y: 2, z: 4, core: 2. Of those that a mesh axis runs over, the one named last changes fastest.
Arguments:
- counts: bfloat16 [2048, 65536], P('rows', 'cols'), may hold values from 0 to 12, as said below
- start_a: float32 [2048, 128], P(('rows', 'cols')), may hold values from -0.4 to 0.4
- start_b: float32 [4096, 128], P(('cols', 'rows')), may hold values from -0.4 to 0.4
- start_c: float32 [16, 128], replicated, may hold values from -0.4 to 0.4
Outputs:
- factor_a: float32 [2048, 128], P(('rows', 'cols'))
- factor_b: float32 [4096, 128], P(('cols', 'rows'))
- factor_c: float32 [16, 128], replicated
The draws below stay inside these ranges and needn't reach their ends.
Inputs may be any that keep to these rules, and one draw needn't show every extreme that they name: counts holds whole numbers.
All inputs are finite; a program needn't handle non-finite values.
Results may differ from the reference program's by a relative error of at most 0.009.
Values may be sent and summed in bfloat16 or wider, within the bound.
A program may use at most 128 MiB of HBM per device.

```python
import math
import jax
import jax.numpy as jnp
from jax import lax

R = 128
K = 16
ITERS = 2
I = 2048
J = 4096


def draw_counts(key, part):
    keys = jax.random.split(key, 4)
    rate_first = jax.random.randint(keys[0], (I, 1, 1), 0, 5)
    rate_second = jax.random.randint(keys[1], (1, J, 1), 0, 5)
    rate_third = jax.random.randint(keys[2], (1, 1, K), 0, 5)
    ceiling = 1 + rate_first + rate_second + rate_third
    values = jax.random.randint(keys[3], (I, J, K), 0, ceiling)
    values = values.at[0, 0, 0].set(12)
    return values.reshape(I, J * K).astype(jnp.float32).astype(jnp.bfloat16)


def shard_levels(key, shape, shards, least, top_value):
    factor_of = 1.0
    for position, blocks in shards:
        steps = jax.random.uniform(jax.random.fold_in(jax.random.fold_in(key, 6), position), (blocks,), jnp.float32, least / len(shards), top_value / len(shards))
        factor_of = factor_of * jnp.repeat(jnp.exp(steps), shape[position] // blocks).reshape((-1,) + (1,) * (len(shape) - 1 - position))
    return factor_of


def setup_inputs(seed: int = 0) -> dict:
    seeds = jax.random.split(jax.random.key(seed), 5)
    counts = draw_counts(jax.random.fold_in(seeds[4], 71), 0)
    start_a = jnp.clip(jax.random.uniform(seeds[1], (I, R), jnp.float32, -0.4, 0.4) * shard_levels(seeds[1], (I, R), ((0, 32),), -0.4, 0.0), -0.4, 0.4)
    start_b = jnp.clip(jax.random.uniform(seeds[2], (J, R), jnp.float32, -0.4, 0.4) * shard_levels(seeds[2], (J, R), ((0, 32),), -0.4, 0.0), -0.4, 0.4)
    start_c = jnp.clip(jax.random.uniform(seeds[3], (K, R), jnp.float32, -0.4, 0.4), -0.4, 0.4)
    return {"counts": counts, "start_a": start_a, "start_b": start_b, "start_c": start_c}


def one_step(counts, whole_a, whole_b, whole_c):
    low_a = whole_a.astype(jnp.bfloat16)
    low_b = whole_b.astype(jnp.bfloat16)
    scaled = (low_b.astype(jnp.float32)[:, None, :] * whole_c[None, :, :]).astype(jnp.bfloat16)
    scaled = scaled.reshape(J * K, R)
    block_rows = math.gcd(I, 256)
    flat = counts.reshape(I // block_rows, block_rows, J * K)
    blocks_a = low_a.reshape(I // block_rows, block_rows, R)

    def visit(mixed, pair):
        values, rows_a = pair
        log_rate = lax.dot_general(rows_a, scaled, (((1,), (1,)), ((), ())), preferred_element_type=jnp.float32)
        residual = (jnp.exp(log_rate) - values.astype(jnp.float32)).astype(jnp.bfloat16)
        grad_rows = jnp.dot(residual, scaled, preferred_element_type=jnp.float32)
        mixed = mixed + lax.dot_general(residual, rows_a, (((0,), (0,)), ((), ())), preferred_element_type=jnp.float32)
        return (mixed, grad_rows)
    mixed, grad_a = lax.scan(visit, jnp.zeros((J * K, R), jnp.float32), (flat, blocks_a))
    grad_a = grad_a.reshape(I, R)
    mixed = mixed.reshape(J, K, R)
    grad_b = lax.optimization_barrier(jnp.sum(mixed * whole_c[None, :, :], axis=1))
    grad_c = lax.optimization_barrier(jnp.sum(mixed * low_b.astype(jnp.float32)[:, None, :], axis=0))
    whole_a = whole_a - 0.3 / math.sqrt(J * K) * grad_a
    whole_b = whole_b - 0.3 / math.sqrt(I * K) * grad_b
    whole_c = whole_c - 0.3 / math.sqrt(I * J) * grad_c
    return (whole_a, whole_b, whole_c)

def reference(counts, start_a, start_b, start_c):
    whole_a, whole_b, whole_c = (start_a, start_b, start_c)
    for iteration in range(ITERS):
        whole_a, whole_b, whole_c = one_step(counts, whole_a, whole_b, whole_c)
    return (whole_a, whole_b, whole_c)
```

```python
import functools
import math

import jax
import jax.numpy as jnp
from jax import lax
from jax.experimental import pallas as pl
from jax.experimental.pallas import tpu as pltpu
from jax.sharding import PartitionSpec as P

ITERS = 2
MESH = pl.DeviceIdType.MESH
F32 = jnp.float32
BF16 = jnp.bfloat16


def kernel(nr, nc, tile, rates, counts_hbm, a_in, b_in, c_in, a_out, b_out, c_out,
           counts, all_a, all_b, send_a, send_b, recv_a, recv_b, part_c, sum_c,
           trans_a, acc_a, acc_c, resid, scaled, grad_b,
           cnt_sem, ag_send, ag_recv, bg_send, bg_recv, ar_send, ar_recv, br_send, br_recv,
           c1_send, c1_recv, c2_send, c2_recv):
    row, col = lax.axis_index("rows"), lax.axis_index("cols")
    rate_a, rate_b, rate_c = rates
    own_a, rank = a_in.shape
    own_b = b_in.shape[0]
    depth = c_in.shape[0]
    tiles = counts.shape[0]
    per = tiles // nr
    width = tile // depth

    def peer(axis, me, n, off):
        p = lax.rem(me + off, n)
        return p, {axis: p}

    def load(t):
        return pltpu.make_async_copy(
            counts_hbm.at[:, pl.ds(pl.multiple_of(t * tile, tile), tile)], counts.at[t], cnt_sem.at[t])

    order = [lax.rem(row + 1 + d, nr) for d in range(nr)]
    for q in order:
        for s in range(per):
            load(q * per + s).start()

    all_a[0, col] = a_in[...].astype(BF16)
    all_b[0, row] = b_in[...].astype(BF16)

    barrier = pltpu.get_barrier_semaphore()
    for off in range(1, nc):
        pl.semaphore_signal(barrier, inc=1, device_id=peer("cols", col, nc, off)[1], device_id_type=MESH)
    for off in range(1, nr):
        pl.semaphore_signal(barrier, inc=1, device_id=peer("rows", row, nr, off)[1], device_id_type=MESH)
    pl.semaphore_wait(barrier, nc + nr - 2)

    def copy(src, dst, ss, rs, dev):
        return pltpu.make_async_remote_copy(
            src_ref=src, dst_ref=dst, send_sem=ss, recv_sem=rs, device_id=dev, device_id_type=MESH)

    class Spread:
        def __init__(self, buf, ss, rs, axis, me, n):
            self.args = (buf, ss, rs, axis, me, n)

        def out(self, off):
            buf, ss, rs, axis, me, n = self.args
            return copy(buf.at[me], buf.at[me], ss.at[off], rs.at[me], peer(axis, me, n, off)[1])

        def start(self):
            for off in range(1, self.args[5]):
                self.out(off).start()

        def wait_recv(self):
            buf, ss, rs, axis, me, n = self.args
            for off in range(1, n):
                p, dev = peer(axis, me, n, off)
                copy(buf.at[p], buf.at[p], ss.at[off], rs.at[p], dev).wait_recv()

        def wait_send(self):
            for off in range(1, self.args[5]):
                self.out(off).wait_send()

    class Scatter:
        def __init__(self, send, recv, ss, rs, axis, me, n):
            self.args = (send, recv, ss, rs, axis, me, n)

        def to(self, p):
            send, recv, ss, rs, axis, me, n = self.args
            return copy(send.at[p], recv.at[me], ss.at[p], rs.at[me], {axis: p})

        def peers(self):
            n = self.args[6]
            return [lax.rem(self.args[5] + off, n) for off in range(1, n)]

        def start(self):
            for p in self.peers():
                self.to(p).start()

        def wait_recv(self):
            send, recv, ss, rs, axis, me, n = self.args
            for p in self.peers():
                copy(send.at[p], recv.at[p], ss.at[p], rs.at[p], {axis: p}).wait_recv()

        def wait_send(self):
            for p in self.peers():
                self.to(p).wait_send()

    pending = []
    local_a, local_b, shared_c = a_in[...], b_in[...], c_in[...]
    gather_a = Spread(all_a.at[0], ag_send.at[0], ag_recv.at[0], "cols", col, nc)
    gather_b = Spread(all_b.at[0], bg_send.at[0], bg_recv.at[0], "rows", row, nr)
    gather_a.start()
    gather_b.start()
    pending += [gather_a, gather_b]

    for it in range(ITERS):
        gather_a.wait_recv()
        gather_b.wait_recv()
        rows_a = all_a[it].reshape(nc * own_a, rank)
        trans_a[...] = rows_a.T
        acc_a[...] = jnp.zeros_like(acc_a)
        acc_c[...] = jnp.zeros_like(acc_c)

        def produce(q, s, slot):
            t = q * per + s
            if it == 0:
                load(t).wait()
            rows_b = all_b[it, q, pl.ds(s * width, width), :].astype(F32)
            wide = (rows_b[:, None, :] * shared_c[None, :, :]).astype(BF16).reshape(tile, rank)
            scaled[slot] = wide
            log_rate = lax.dot_general(
                all_a[it].reshape(nc * own_a, rank), wide, (((1,), (1,)), ((), ())), preferred_element_type=F32)
            resid[slot] = (jnp.exp(log_rate) - counts[t].astype(F32)).astype(BF16)

        def consume(q, s, slot):
            acc_a[...] += jnp.dot(resid[slot], scaled[slot], preferred_element_type=F32)
            mixed = jnp.dot(trans_a[...], resid[slot], preferred_element_type=F32).T
            mixed = mixed.reshape(width, depth, rank)
            rows_b = all_b[it, q, pl.ds(s * width, width), :].astype(F32)
            grad_b[pl.ds(s * width, width), :] = jnp.sum(mixed * shared_c[None, :, :], axis=1)
            acc_c[...] += jnp.sum(mixed * rows_b[:, None, :], axis=0)

        scatter_b = Scatter(send_b.at[it], recv_b.at[it], br_send.at[it], br_recv.at[it], "rows", row, nr)
        produce(order[0], 0, 0)

        def step(d, carry):
            q = lax.rem(row + 1 + d, nr)
            for s in range(per):
                if s + 1 < per:
                    produce(q, s + 1, (s + 1) % 2)
                else:
                    @pl.when(d < nr - 1)
                    def _():
                        produce(lax.rem(q + 1, nr), 0, (s + 1) % 2)
                consume(q, s, s % 2)
            send_b[it, q] = grad_b[...].astype(BF16)

            @pl.when(d < nr - 1)
            def _():
                scatter_b.to(q).start()

            return carry

        lax.fori_loop(0, nr, step, 0)
        pending.append(scatter_b)

        for p in range(nc):
            send_a[it, p] = acc_a[pl.ds(p * own_a, own_a), :].astype(BF16)
        part_c[it, col] = acc_c[...].astype(BF16)
        scatter_a = Scatter(send_a.at[it], recv_a.at[it], ar_send.at[it], ar_recv.at[it], "cols", col, nc)
        scatter_a.start()
        cols_c = Spread(part_c.at[it], c1_send.at[it], c1_recv.at[it], "cols", col, nc)
        cols_c.start()
        pending += [scatter_a, cols_c]

        scatter_b.wait_recv()
        recv_b[it, row] = jnp.zeros((own_b, rank), BF16)
        total_b = grad_b[...] + jnp.sum(recv_b[it].astype(F32), axis=0)
        local_b = local_b - rate_b * total_b
        last = it == ITERS - 1
        if last:
            b_out[...] = local_b
        else:
            all_b[it + 1, row] = local_b.astype(BF16)
            gather_b = Spread(all_b.at[it + 1], bg_send.at[it + 1], bg_recv.at[it + 1], "rows", row, nr)
            gather_b.start()
            pending.append(gather_b)

        scatter_a.wait_recv()
        recv_a[it, col] = jnp.zeros((own_a, rank), BF16)
        own_rows = pl.ds(pl.multiple_of(col * own_a, own_a), own_a)
        total_a = acc_a[own_rows, :] + jnp.sum(recv_a[it].astype(F32), axis=0)
        local_a = local_a - rate_a * total_a
        if last:
            a_out[...] = local_a
        else:
            all_a[it + 1, col] = local_a.astype(BF16)
            gather_a = Spread(all_a.at[it + 1], ag_send.at[it + 1], ag_recv.at[it + 1], "cols", col, nc)
            gather_a.start()
            pending.append(gather_a)

        cols_c.wait_recv()
        sum_c[it, row] = jnp.sum(part_c[it].astype(F32), axis=0)
        rows_c = Spread(sum_c.at[it], c2_send.at[it], c2_recv.at[it], "rows", row, nr)
        rows_c.start()
        pending.append(rows_c)
        rows_c.wait_recv()
        shared_c = shared_c - rate_c * jnp.sum(sum_c[it], axis=0)
        if last:
            c_out[...] = shared_c

    for group in pending:
        group.wait_send()


def local(nr, nc, counts, start_a, start_b, start_c):
    rows_here, flat_width = counts.shape
    own_a, rank = start_a.shape
    own_b = start_b.shape[0]
    depth = start_c.shape[0]
    cols_here = flat_width // depth
    total_i, total_j = rows_here * nr, cols_here * nc
    rates = (0.3 / math.sqrt(total_j * depth), 0.3 / math.sqrt(total_i * depth), 0.3 / math.sqrt(total_i * total_j))
    tile = 512
    tiles = flat_width // tile
    vmem = pl.BlockSpec(memory_space=pltpu.VMEM)
    dma = pltpu.SemaphoreType.DMA
    return pl.pallas_call(
        functools.partial(kernel, nr, nc, tile, rates),
        out_shape=[jax.ShapeDtypeStruct(x.shape, F32) for x in (start_a, start_b, start_c)],
        in_specs=[pl.BlockSpec(memory_space=pl.ANY), vmem, vmem, vmem],
        out_specs=[vmem] * 3,
        scratch_shapes=[
            pltpu.VMEM((tiles, rows_here, tile), BF16),
            pltpu.VMEM((ITERS, nc, own_a, rank), BF16),
            pltpu.VMEM((ITERS, nr, own_b, rank), BF16),
            pltpu.VMEM((ITERS, nc, own_a, rank), BF16),
            pltpu.VMEM((ITERS, nr, own_b, rank), BF16),
            pltpu.VMEM((ITERS, nc, own_a, rank), BF16),
            pltpu.VMEM((ITERS, nr, own_b, rank), BF16),
            pltpu.VMEM((ITERS, nc, depth, rank), BF16),
            pltpu.VMEM((ITERS, nr, depth, rank), F32),
            pltpu.VMEM((rank, rows_here), BF16),
            pltpu.VMEM((rows_here, rank), F32),
            pltpu.VMEM((depth, rank), F32),
            pltpu.VMEM((2, rows_here, tile), BF16),
            pltpu.VMEM((2, tile, rank), BF16),
            pltpu.VMEM((own_b, rank), F32),
            dma((tiles,)),
            dma((ITERS, nc)), dma((ITERS, nc)), dma((ITERS, nr)), dma((ITERS, nr)),
            dma((ITERS, nc)), dma((ITERS, nc)), dma((ITERS, nr)), dma((ITERS, nr)),
            dma((ITERS, nc)), dma((ITERS, nc)), dma((ITERS, nr)), dma((ITERS, nr)),
        ],
        compiler_params=pltpu.CompilerParams(
            collective_id=0, has_side_effects=True, vmem_limit_bytes=56 * 1024 * 1024),
    )(counts, start_a, start_b, start_c)


def solution(mesh):
    nr, nc = mesh.shape["rows"], mesh.shape["cols"]
    placed = (P("rows", "cols"), P(("rows", "cols"), None), P(("cols", "rows"), None), P())
    return jax.shard_map(
        functools.partial(local, nr, nc),
        mesh=mesh,
        in_specs=placed,
        out_specs=(P(("rows", "cols"), None), P(("cols", "rows"), None), P()),
        check_vma=False,
    )
```

```python
import functools
import math

import jax
import jax.numpy as jnp
from jax import lax
from jax.experimental import pallas as pl
from jax.experimental.pallas import tpu as pltpu
from jax.sharding import PartitionSpec as P

ITERS = 2
MESH = pl.DeviceIdType.MESH
F32 = jnp.float32
BF16 = jnp.bfloat16


def kernel(nr, nc, tile, rates, counts_hbm, a_in, b_in, c_in, a_out, b_out, c_out,
           counts, all_a, all_b, send_a, send_b, recv_a, recv_b, part_c, sum_c,
           held_a, trans_a, acc_a, acc_c, resid, scaled, mixed_t, grad_b,
           cnt_sem, ag_send, ag_recv, bg_send, bg_recv, ar_send, ar_recv, br_send, br_recv,
           c1_send, c1_recv, c2_send, c2_recv):
    row, col = lax.axis_index("rows"), lax.axis_index("cols")
    rate_a, rate_b, rate_c = rates
    own_a, rank = a_in.shape
    own_b = b_in.shape[0]
    depth = c_in.shape[0]
    tiles = counts.shape[1]
    per = tiles // nr
    width = tile // depth

    half = nc // 2
    near, spot = lax.div(col, half), lax.rem(col, half)
    near_peers = [near * half + lax.rem(spot + off, half) for off in range(1, half)]
    far_peers = [(1 - near) * half + lax.rem(spot + off, half) for off in range(half)]
    col_peers = near_peers + far_peers
    row_peers = [lax.rem(row + off, nr) for off in range(1, nr)]
    half_rows = half * own_a

    def load(h, t):
        return pltpu.make_async_copy(
            counts_hbm.at[pl.ds(pl.multiple_of(h * half_rows, half_rows), half_rows),
                          pl.ds(pl.multiple_of(t * tile, tile), tile)],
            counts.at[h, t], cnt_sem.at[h, t])

    def chunk(side, d):
        return lax.rem(row + side + d, nr)

    sides = (near, 1 - near)
    for side in range(2):
        for d in range(nr):
            for s in range(per):
                load(sides[side], chunk(side, d) * per + s).start()

    all_a[0, col] = a_in[...].astype(BF16)
    all_b[0, row] = b_in[...].astype(BF16)

    barrier = pltpu.get_barrier_semaphore()
    for p in col_peers:
        pl.semaphore_signal(barrier, inc=1, device_id={"cols": p}, device_id_type=MESH)
    for p in row_peers:
        pl.semaphore_signal(barrier, inc=1, device_id={"rows": p}, device_id_type=MESH)
    pl.semaphore_wait(barrier, nc + nr - 2)

    class Exchange:
        def __init__(self, send, recv, ss, rs, axis, me):
            self.args = (send, recv, ss, rs, axis, me)

        def to(self, p):
            send, recv, ss, rs, axis, me = self.args
            return pltpu.make_async_remote_copy(
                src_ref=recv.at[me] if send is None else send.at[p], dst_ref=recv.at[me],
                send_sem=ss.at[p], recv_sem=rs.at[me], device_id={axis: p}, device_id_type=MESH)

        def start(self, peers):
            for p in peers:
                self.to(p).start()

        def wait_recv(self, peers):
            send, recv, ss, rs, axis, me = self.args
            for p in peers:
                pltpu.make_async_remote_copy(
                    src_ref=recv.at[p], dst_ref=recv.at[p], send_sem=ss.at[p], recv_sem=rs.at[p],
                    device_id={axis: p}, device_id_type=MESH).wait_recv()

        def wait_send(self, peers):
            for p in peers:
                self.to(p).wait_send()

    pending = []
    local_a, local_b, shared_c = a_in[...], b_in[...], c_in[...]

    def gather(it):
        return (Exchange(None, all_a.at[it], ag_send.at[it], ag_recv.at[it], "cols", col),
                Exchange(None, all_b.at[it], bg_send.at[it], bg_recv.at[it], "rows", row))

    gather_a, gather_b = gather(0)
    gather_b.start(row_peers)
    gather_a.start(col_peers)

    for it in range(ITERS):
        pending += [(gather_a, col_peers), (gather_b, row_peers)]
        scatter_a = Exchange(send_a.at[it], recv_a.at[it], ar_send.at[it], ar_recv.at[it], "cols", col)
        scatter_b = Exchange(send_b.at[it], recv_b.at[it], br_send.at[it], br_recv.at[it], "rows", row)
        cols_c = Exchange(None, part_c.at[it], c1_send.at[it], c1_recv.at[it], "cols", col)
        rows_c = Exchange(None, sum_c.at[it], c2_send.at[it], c2_recv.at[it], "rows", row)
        pending += [(scatter_a, col_peers), (scatter_b, row_peers), (cols_c, col_peers), (rows_c, row_peers)]
        acc_a[...] = jnp.zeros_like(acc_a)
        acc_c[...] = jnp.zeros_like(acc_c)

        for side in range(2):
            h = sides[side]
            gather_a.wait_recv((near_peers, far_peers)[side])
            rows_a = all_a[it, pl.ds(h * half, half)].reshape(half_rows, rank)
            held_a[...] = rows_a
            trans_a[...] = rows_a.T

            def produce(q, s, slot):
                t = q * per + s
                if it == 0:
                    load(h, t).wait()
                if side == 0:
                    rows_b = all_b[it, q, pl.ds(s * width, width), :].astype(F32)
                    scaled[t] = (rows_b[:, None, :] * shared_c[None, :, :]).astype(BF16).reshape(tile, rank)
                log_rate = lax.dot_general(
                    held_a[...], scaled[t], (((1,), (1,)), ((), ())), preferred_element_type=F32)
                resid[slot] = (jnp.exp(log_rate) - counts[h, t].astype(F32)).astype(BF16)

            def consume(q, s, slot):
                t = q * per + s
                acc_a[h] += jnp.dot(resid[slot], scaled[t], preferred_element_type=F32)
                turned = jnp.dot(trans_a[...], resid[slot], preferred_element_type=F32)
                if side == 0:
                    mixed_t[t] = turned
                    return
                mixed = (mixed_t[t] + turned).T.reshape(width, depth, rank)
                rows_b = all_b[it, q, pl.ds(s * width, width), :].astype(F32)
                grad_b[pl.ds(s * width, width), :] = jnp.sum(mixed * shared_c[None, :, :], axis=1)
                acc_c[...] += jnp.sum(mixed * rows_b[:, None, :], axis=0)

            def step(d, carry):
                q = chunk(side, d)
                for s in range(per):
                    if s + 1 < per:
                        produce(q, s + 1, (s + 1) % 2)
                    else:
                        @pl.when(d < nr - 1)
                        def _():
                            q_next = chunk(side, d + 1)
                            if side == 0:
                                gather_b.wait_recv([q_next])
                            produce(q_next, 0, 0)
                    consume(q, s, s % 2)
                if side == 1:
                    send_b[it, q] = grad_b[...].astype(BF16)

                    @pl.when(d < nr - 1)
                    def _():
                        scatter_b.start([q])

                return carry

            produce(chunk(side, 0), 0, 0)
            lax.fori_loop(0, nr, step, 0)

            if side == 1:
                part_c[it, col] = acc_c[...].astype(BF16)
                cols_c.start(far_peers + near_peers)
            for k in range(half):
                send_a[it, h * half + k] = acc_a[h, pl.ds(k * own_a, own_a), :].astype(BF16)
            scatter_a.start((near_peers, far_peers)[side])

        last = it == ITERS - 1
        if not last:
            gather_a, gather_b = gather(it + 1)

        scatter_b.wait_recv(row_peers)
        recv_b[it, row] = jnp.zeros((own_b, rank), BF16)
        total_b = grad_b[...] + jnp.sum(recv_b[it].astype(F32), axis=0)
        local_b = local_b - rate_b * total_b
        if last:
            b_out[...] = local_b
        else:
            all_b[it + 1, row] = local_b.astype(BF16)
            gather_b.start(row_peers)

        cols_c.wait_recv(col_peers)
        sum_c[it, row] = jnp.sum(part_c[it].astype(F32), axis=0)
        rows_c.start(row_peers)

        scatter_a.wait_recv(col_peers)
        recv_a[it, col] = jnp.zeros((own_a, rank), BF16)
        total_a = acc_a[near, pl.ds(pl.multiple_of(spot * own_a, own_a), own_a), :] + jnp.sum(recv_a[it].astype(F32), axis=0)
        local_a = local_a - rate_a * total_a
        if last:
            a_out[...] = local_a
        else:
            all_a[it + 1, col] = local_a.astype(BF16)
            gather_a.start(col_peers)

        rows_c.wait_recv(row_peers)
        shared_c = shared_c - rate_c * jnp.sum(sum_c[it], axis=0)
        if last:
            c_out[...] = shared_c

    for group, peers in pending:
        group.wait_send(peers)


def finish(a, b, c, a_out, b_out, c_out):
    a_out[...] = a[...]
    b_out[...] = b[...]
    c_out[...] = c[...]


def local(nr, nc, counts, start_a, start_b, start_c):
    rows_here, flat_width = counts.shape
    own_a, rank = start_a.shape
    own_b = start_b.shape[0]
    depth = start_c.shape[0]
    cols_here = flat_width // depth
    total_i, total_j = rows_here * nr, cols_here * nc
    rates = (0.3 / math.sqrt(total_j * depth), 0.3 / math.sqrt(total_i * depth), 0.3 / math.sqrt(total_i * total_j))
    tile = 512
    tiles = flat_width // tile
    vmem = pl.BlockSpec(memory_space=pltpu.VMEM)
    dma = pltpu.SemaphoreType.DMA
    outs = [jax.ShapeDtypeStruct(x.shape, F32) for x in (start_a, start_b, start_c)]
    half_rows = rows_here // 2
    found = pl.pallas_call(
        functools.partial(kernel, nr, nc, tile, rates),
        out_shape=outs,
        in_specs=[pl.BlockSpec(memory_space=pl.ANY), vmem, vmem, vmem],
        out_specs=[vmem] * 3,
        scratch_shapes=[
            pltpu.VMEM((2, tiles, half_rows, tile), BF16),
            pltpu.VMEM((ITERS, nc, own_a, rank), BF16),
            pltpu.VMEM((ITERS, nr, own_b, rank), BF16),
            pltpu.VMEM((ITERS, nc, own_a, rank), BF16),
            pltpu.VMEM((ITERS, nr, own_b, rank), BF16),
            pltpu.VMEM((ITERS, nc, own_a, rank), BF16),
            pltpu.VMEM((ITERS, nr, own_b, rank), BF16),
            pltpu.VMEM((ITERS, nc, depth, rank), BF16),
            pltpu.VMEM((ITERS, nr, depth, rank), F32),
            pltpu.VMEM((half_rows, rank), BF16),
            pltpu.VMEM((rank, half_rows), BF16),
            pltpu.VMEM((2, half_rows, rank), F32),
            pltpu.VMEM((depth, rank), F32),
            pltpu.VMEM((2, half_rows, tile), BF16),
            pltpu.VMEM((tiles, tile, rank), BF16),
            pltpu.VMEM((tiles, rank, tile), F32),
            pltpu.VMEM((own_b, rank), F32),
            dma((2, tiles)),
            dma((ITERS, nc)), dma((ITERS, nc)), dma((ITERS, nr)), dma((ITERS, nr)),
            dma((ITERS, nc)), dma((ITERS, nc)), dma((ITERS, nr)), dma((ITERS, nr)),
            dma((ITERS, nc)), dma((ITERS, nc)), dma((ITERS, nr)), dma((ITERS, nr)),
        ],
        compiler_params=pltpu.CompilerParams(
            collective_id=0, has_side_effects=True, vmem_limit_bytes=56 * 1024 * 1024),
    )(counts, start_a, start_b, start_c)
    return pl.pallas_call(finish, out_shape=outs, in_specs=[vmem] * 3, out_specs=[vmem] * 3)(*found)


def solution(mesh):
    nr, nc = mesh.shape["rows"], mesh.shape["cols"]
    placed = (P("rows", "cols"), P(("rows", "cols"), None), P(("cols", "rows"), None), P())
    return jax.shard_map(
        functools.partial(local, nr, nc),
        mesh=mesh,
        in_specs=placed,
        out_specs=(P(("rows", "cols"), None), P(("cols", "rows"), None), P()),
        check_vma=False,
    )
```

```python
import functools
import math

import jax
import jax.numpy as jnp
from jax import lax
from jax.experimental import pallas as pl
from jax.experimental.pallas import tpu as pltpu
from jax.sharding import PartitionSpec as P

ITERS = 2
MESH = pl.DeviceIdType.MESH
F32 = jnp.float32
BF16 = jnp.bfloat16


def kernel(nr, nc, tile, rates, counts_hbm, a_in, b_in, c_in, a_out, b_out, c_out,
           counts, all_a, all_b, send_a, send_b, recv_a, recv_b, part_c, sum_c,
           held_a, trans_a, acc_a, acc_c, resid, scaled, mixed_t, grad_b,
           cnt_sem, ag_send, ag_recv, bg_send, bg_recv, ar_send, ar_recv, br_send, br_recv,
           c1_send, c1_recv, c2_send, c2_recv):
    row, col = lax.axis_index("rows"), lax.axis_index("cols")
    rate_a, rate_b, rate_c = rates
    own_a, rank = a_in.shape
    own_b = b_in.shape[0]
    depth = c_in.shape[0]
    tiles = counts.shape[1]
    per = tiles // nr
    width = tile // depth

    half = nc // 2
    near, spot = lax.div(col, half), lax.rem(col, half)
    near_peers = [near * half + lax.rem(spot + off, half) for off in range(1, half)]
    far_peers = [(1 - near) * half + lax.rem(spot + off, half) for off in range(half)]
    col_peers = near_peers + far_peers
    row_peers = [lax.rem(row + off, nr) for off in range(1, nr)]
    half_rows = half * own_a

    def load(h, t):
        return pltpu.make_async_copy(
            counts_hbm.at[pl.ds(pl.multiple_of(h * half_rows, half_rows), half_rows),
                          pl.ds(pl.multiple_of(t * tile, tile), tile)],
            counts.at[h, t], cnt_sem.at[h, t])

    def chunk(side, d):
        return lax.rem(row + side + d, nr)

    sides = (near, 1 - near)
    for side in range(2):
        for d in range(nr):
            for s in range(per):
                load(sides[side], chunk(side, d) * per + s).start()

    all_a[0, col] = a_in[...].astype(BF16)
    all_b[0, row] = b_in[...].astype(BF16)

    barrier = pltpu.get_barrier_semaphore()
    for p in col_peers:
        pl.semaphore_signal(barrier, inc=1, device_id={"cols": p}, device_id_type=MESH)
    for p in row_peers:
        pl.semaphore_signal(barrier, inc=1, device_id={"rows": p}, device_id_type=MESH)
    pl.semaphore_wait(barrier, nc + nr - 2)

    class Exchange:
        def __init__(self, send, recv, ss, rs, axis, me):
            self.args = (send, recv, ss, rs, axis, me)

        def to(self, p):
            send, recv, ss, rs, axis, me = self.args
            return pltpu.make_async_remote_copy(
                src_ref=recv.at[me] if send is None else send.at[p], dst_ref=recv.at[me],
                send_sem=ss.at[p], recv_sem=rs.at[me], device_id={axis: p}, device_id_type=MESH)

        def start(self, peers):
            for p in peers:
                self.to(p).start()

        def wait_recv(self, peers):
            send, recv, ss, rs, axis, me = self.args
            for p in peers:
                pltpu.make_async_remote_copy(
                    src_ref=recv.at[p], dst_ref=recv.at[p], send_sem=ss.at[p], recv_sem=rs.at[p],
                    device_id={axis: p}, device_id_type=MESH).wait_recv()

        def wait_send(self, peers):
            for p in peers:
                self.to(p).wait_send()

    pending = []
    local_a, local_b, shared_c = a_in[...], b_in[...], c_in[...]

    def gather(it):
        return (Exchange(None, all_a.at[it], ag_send.at[it], ag_recv.at[it], "cols", col),
                Exchange(None, all_b.at[it], bg_send.at[it], bg_recv.at[it], "rows", row))

    gather_a, gather_b = gather(0)
    gather_b.start(row_peers)
    gather_a.start(col_peers)

    for it in range(ITERS):
        pending += [(gather_a, col_peers), (gather_b, row_peers)]
        scatter_a = Exchange(send_a.at[it], recv_a.at[it], ar_send.at[it], ar_recv.at[it], "cols", col)
        scatter_b = Exchange(send_b.at[it], recv_b.at[it], br_send.at[it], br_recv.at[it], "rows", row)
        cols_c = Exchange(None, part_c.at[it], c1_send.at[it], c1_recv.at[it], "cols", col)
        rows_c = Exchange(None, sum_c.at[it], c2_send.at[it], c2_recv.at[it], "rows", row)
        pending += [(scatter_a, col_peers), (scatter_b, row_peers), (cols_c, col_peers), (rows_c, row_peers)]
        acc_a[...] = jnp.zeros_like(acc_a)
        acc_c[...] = jnp.zeros_like(acc_c)

        for side in range(2):
            h = sides[side]
            gather_a.wait_recv((near_peers, far_peers)[side])
            rows_a = all_a[it, pl.ds(h * half, half)].reshape(half_rows, rank)
            held_a[...] = rows_a
            trans_a[...] = rows_a.T

            def produce(q, s, slot):
                t = q * per + s
                if side == 0:
                    rows_b = all_b[it, q, pl.ds(s * width, width), :].astype(F32)
                    scaled[t] = (rows_b[:, None, :] * shared_c[None, :, :]).astype(BF16).reshape(tile, rank)
                log_rate = lax.dot_general(
                    held_a[...], scaled[t], (((1,), (1,)), ((), ())), preferred_element_type=F32)
                resid[slot] = (jnp.exp(log_rate) - counts[h, t].astype(F32)).astype(BF16)

            def consume(q, s, slot):
                t = q * per + s
                acc_a[h] += jnp.dot(resid[slot], scaled[t], preferred_element_type=F32)
                turned = jnp.dot(trans_a[...], resid[slot], preferred_element_type=F32)
                if side == 0:
                    mixed_t[t] = turned
                    return
                mixed = (mixed_t[t] + turned).T.reshape(width, depth, rank)
                rows_b = all_b[it, q, pl.ds(s * width, width), :].astype(F32)
                grad_b[pl.ds(s * width, width), :] = jnp.sum(mixed * shared_c[None, :, :], axis=1)
                acc_c[...] += jnp.sum(mixed * rows_b[:, None, :], axis=0)

            def ready(d):
                q = chunk(side, d)
                if it == 0:
                    for s in range(per):
                        load(h, q * per + s).wait()
                return q

            def step(d, carry):
                q, q_next = chunk(side, d), chunk(side, d + 1)
                if side == 0 or it == 0:
                    @pl.when(d < nr - 1)
                    def _():
                        ready(d + 1)
                        if side == 0:
                            gather_b.wait_recv([q_next])
                for s in range(per):
                    if s + 1 < per:
                        produce(q, s + 1, (s + 1) % 2)
                    else:
                        produce(q_next, 0, 0)
                    consume(q, s, s % 2)
                if side == 1:
                    send_b[it, q] = grad_b[...].astype(BF16)

                    @pl.when(d < nr - 1)
                    def _():
                        scatter_b.start([q])

                return carry

            produce(ready(0), 0, 0)
            lax.fori_loop(0, nr, step, 0)

            if side == 1:
                part_c[it, col] = acc_c[...].astype(BF16)
                cols_c.start(far_peers + near_peers)
            for k in range(half):
                send_a[it, h * half + k] = acc_a[h, pl.ds(k * own_a, own_a), :].astype(BF16)
            scatter_a.start((near_peers, far_peers)[side])

        last = it == ITERS - 1
        if not last:
            gather_a, gather_b = gather(it + 1)

        scatter_b.wait_recv(row_peers)
        recv_b[it, row] = jnp.zeros((own_b, rank), BF16)
        total_b = grad_b[...] + jnp.sum(recv_b[it].astype(F32), axis=0)
        local_b = local_b - rate_b * total_b
        if last:
            b_out[...] = local_b
        else:
            all_b[it + 1, row] = local_b.astype(BF16)
            gather_b.start(row_peers)

        cols_c.wait_recv(col_peers)
        sum_c[it, row] = jnp.sum(part_c[it].astype(F32), axis=0)
        rows_c.start(row_peers)

        scatter_a.wait_recv(col_peers)
        recv_a[it, col] = jnp.zeros((own_a, rank), BF16)
        total_a = acc_a[near, pl.ds(pl.multiple_of(spot * own_a, own_a), own_a), :] + jnp.sum(recv_a[it].astype(F32), axis=0)
        local_a = local_a - rate_a * total_a
        if last:
            a_out[...] = local_a
        else:
            all_a[it + 1, col] = local_a.astype(BF16)
            gather_a.start(col_peers)

        rows_c.wait_recv(row_peers)
        shared_c = shared_c - rate_c * jnp.sum(sum_c[it], axis=0)
        if last:
            c_out[...] = shared_c

    for group, peers in pending:
        group.wait_send(peers)


def finish(a, b, c, a_out, b_out, c_out):
    a_out[...] = a[...]
    b_out[...] = b[...]
    c_out[...] = c[...]


def local(nr, nc, counts, start_a, start_b, start_c):
    rows_here, flat_width = counts.shape
    own_a, rank = start_a.shape
    own_b = start_b.shape[0]
    depth = start_c.shape[0]
    cols_here = flat_width // depth
    total_i, total_j = rows_here * nr, cols_here * nc
    rates = (0.3 / math.sqrt(total_j * depth), 0.3 / math.sqrt(total_i * depth), 0.3 / math.sqrt(total_i * total_j))
    tile = 512
    tiles = flat_width // tile
    vmem = pl.BlockSpec(memory_space=pltpu.VMEM)
    dma = pltpu.SemaphoreType.DMA
    outs = [jax.ShapeDtypeStruct(x.shape, F32) for x in (start_a, start_b, start_c)]
    half_rows = rows_here // 2
    found = pl.pallas_call(
        functools.partial(kernel, nr, nc, tile, rates),
        out_shape=outs,
        in_specs=[pl.BlockSpec(memory_space=pl.ANY), vmem, vmem, vmem],
        out_specs=[vmem] * 3,
        scratch_shapes=[
            pltpu.VMEM((2, tiles, half_rows, tile), BF16),
            pltpu.VMEM((ITERS, nc, own_a, rank), BF16),
            pltpu.VMEM((ITERS, nr, own_b, rank), BF16),
            pltpu.VMEM((ITERS, nc, own_a, rank), BF16),
            pltpu.VMEM((ITERS, nr, own_b, rank), BF16),
            pltpu.VMEM((ITERS, nc, own_a, rank), BF16),
            pltpu.VMEM((ITERS, nr, own_b, rank), BF16),
            pltpu.VMEM((ITERS, nc, depth, rank), BF16),
            pltpu.VMEM((ITERS, nr, depth, rank), F32),
            pltpu.VMEM((half_rows, rank), BF16),
            pltpu.VMEM((rank, half_rows), BF16),
            pltpu.VMEM((2, half_rows, rank), F32),
            pltpu.VMEM((depth, rank), F32),
            pltpu.VMEM((2, half_rows, tile), BF16),
            pltpu.VMEM((tiles, tile, rank), BF16),
            pltpu.VMEM((tiles, rank, tile), F32),
            pltpu.VMEM((own_b, rank), F32),
            dma((2, tiles)),
            dma((ITERS, nc)), dma((ITERS, nc)), dma((ITERS, nr)), dma((ITERS, nr)),
            dma((ITERS, nc)), dma((ITERS, nc)), dma((ITERS, nr)), dma((ITERS, nr)),
            dma((ITERS, nc)), dma((ITERS, nc)), dma((ITERS, nr)), dma((ITERS, nr)),
        ],
        compiler_params=pltpu.CompilerParams(
            collective_id=0, has_side_effects=True, vmem_limit_bytes=56 * 1024 * 1024),
    )(counts, start_a, start_b, start_c)
    return pl.pallas_call(finish, out_shape=outs, in_specs=[vmem] * 3, out_specs=[vmem] * 3)(*found)


def solution(mesh):
    nr, nc = mesh.shape["rows"], mesh.shape["cols"]
    placed = (P("rows", "cols"), P(("rows", "cols"), None), P(("cols", "rows"), None), P())
    return jax.shard_map(
        functools.partial(local, nr, nc),
        mesh=mesh,
        in_specs=placed,
        out_specs=(P(("rows", "cols"), None), P(("cols", "rows"), None), P()),
        check_vma=False,
    )
```
